32 devices in a mesh: occ: 16 (over z, y, x), blk: 2 (over core).
Axes of the slice: x: 2, y: 2, z: 4, core: 2. Of those that a mesh axis runs over, the one named last changes fastest.
Arguments:
- integrals: bfloat16 [20480, 16, 240], P(('occ', 'blk')), may hold values from -0.7 to 0.7
- domain_transforms: bfloat16 [32, 24, 24], replicated, may hold values from -1.25 to 1.25
- domain_lists: int32 [16, 2, 5], replicated, may hold values from 0 to 31, all different within a row
- occ_energies: float32 [16, 2, 1], P('occ'), may hold values from -1.5 to -0.4
- virt_energies: float32 [32, 24], replicated, may hold values from 0.3 to 2.5
- pair_pattern: int32 [16, 2, 2], P('occ'), may hold values from 0 to 1, as said below
Outputs:
- gradient_gamma: bfloat16 [20480, 16, 240], P(('occ', 'blk'))
The draws below stay inside these ranges and needn't reach their ends.
Inputs may be any that keep to these rules, and one draw needn't show every extreme that they name: `domain_lists`: the 5 virtual blocks of each occupied block are distinct. `pair_pattern`: symmetric in its last two dimensions, with ones on the diagonal.
All inputs are finite; a program needn't handle non-finite values.
Results may differ from the reference program's by a relative error of at most 0.0049.
Values may be sent and summed in bfloat16 or wider, within the bound.
A program may use at most 128 MiB of HBM per device.

```python
import jax
import jax.numpy as jnp
from jax import lax

NAUX = 20480
VB = 24
NDOM = 5
OB = 1
NGRP = 16
NB = 2
NVB = 32


def draw_integrals(key, part):
    base_key, row_key, col_key = jax.random.split(key, 3)
    shape_full = (NAUX, NGRP, NB * OB * NDOM, VB)
    noise = jnp.clip(jax.random.normal(base_key, shape_full, jnp.float32), -5.0, 5.0)
    row_scale = jnp.exp(jax.random.uniform(row_key, (NAUX, 1, 1, 1), jnp.float32, -1.15, 1.15))
    col_scale = jnp.exp(jax.random.uniform(col_key, (1, NGRP, NB * OB * NDOM, 1), jnp.float32, -0.35, 0.35))
    values = 0.03 * row_scale * col_scale * noise
    return values.reshape(NAUX, NGRP, NB * OB * NDOM * VB).astype(jnp.bfloat16)


def draw_pair_pattern(key, part):
    level_key, entry_key = jax.random.split(key)
    levels = jax.random.randint(level_key, (NGRP, 1, 1), 0, 9)
    entries = jax.random.randint(entry_key, (NGRP, NB, NB), 0, 8)
    first = lax.broadcasted_iota(jnp.int32, (NGRP, NB, NB), 1)
    second = lax.broadcasted_iota(jnp.int32, (NGRP, NB, NB), 2)
    mirrored = jnp.where(first < second, entries, jnp.swapaxes(entries, 1, 2))
    linked = (mirrored < levels).astype(jnp.int32)
    return jnp.where(first == second, 1, linked).astype(jnp.int32)


def shard_levels(key, shape, cuts, least, top_value):
    loudness = 1.0
    for position, shards_of in cuts:
        steps = jax.random.uniform(jax.random.fold_in(jax.random.fold_in(key, 6), position), (shards_of,), jnp.float32, least / len(cuts), top_value / len(cuts))
        loudness = loudness * jnp.repeat(jnp.exp(steps), shape[position] // shards_of).reshape((-1,) + (1,) * (len(shape) - 1 - position))
    return loudness


def picks_of(own_key, rows, amount, top, lift):
    order = jax.random.permutation(jax.random.fold_in(own_key, 1), amount)
    favour = order
    for power in range(3):
        favour = favour * favour // amount
    favour = favour * lift // amount
    chance = jax.random.randint(jax.random.fold_in(own_key, 2), (rows, amount), 0, 4096) + favour
    fixed_rows = jax.random.permutation(jax.random.fold_in(own_key, 3), rows)[jnp.arange(amount) % rows]
    chance = jnp.where(jnp.arange(rows)[:, None] == fixed_rows[None, :], 1 << 14, chance)
    score = chance * amount + jnp.arange(amount)
    return lax.top_k(score.astype(jnp.int32), top)[1].astype(jnp.int32)


def scatter_about(stream_key, dims, spread, most, kind=jnp.bfloat16):
    return jnp.clip(spread * jax.random.normal(stream_key, dims, jnp.float32), -most, most).astype(kind)


def setup_inputs(seed: int = 0) -> dict:
    keys = jax.random.split(jax.random.key(seed), 7)
    integrals = draw_integrals(jax.random.fold_in(keys[6], 71), 0)
    domain_transforms = scatter_about(keys[1], (NVB, VB, VB), VB ** -0.5, 1.25)
    domain_lists = picks_of(keys[2], NGRP * NB, NVB, NDOM, 0).reshape((NGRP, NB, NDOM))
    occ_energies = jnp.clip(-1.5 + 1.1 * jax.random.uniform(keys[3], (NGRP, NB, OB), jnp.float32) ** shard_levels(keys[3], (NGRP, NB, OB), ((0, 16),), -0.2, 0.2), -1.5, -0.4)
    virt_energies = jnp.clip(jax.random.uniform(keys[4], (NVB, VB), jnp.float32, 0.3, 2.5), 0.3, 2.5)
    pair_pattern = draw_pair_pattern(jax.random.fold_in(keys[6], 71), 0)
    return dict(integrals=integrals, domain_transforms=domain_transforms, domain_lists=domain_lists, occ_energies=occ_energies, virt_energies=virt_energies, pair_pattern=pair_pattern)


def one_group(integrals, domain_transforms, domain_lists, occ_energies, virt_energies, pair_pattern, group):
    raw_rows = lax.dynamic_index_in_dim(integrals, group, 1, keepdims=False)
    lists_now = lax.dynamic_index_in_dim(domain_lists, group, 0, keepdims=False)
    chosen = jnp.take(domain_transforms, lists_now, axis=0).astype(jnp.float32)
    block_count = lists_now.shape[0]
    width_all = raw_rows.shape[1]
    shaped = raw_rows.astype(jnp.float32).reshape(NAUX, block_count, OB, NDOM, VB)
    fitted = jnp.einsum("pbomu,bmuv->pbomv", shaped, chosen)
    fitted = fitted.astype(jnp.bfloat16).reshape(NAUX, width_all)
    block_virt = jnp.take(virt_energies, lists_now, axis=0)
    occ_now = lax.dynamic_index_in_dim(occ_energies, group, 0, keepdims=False)
    col_energy = (occ_now[:, :, None, None] - block_virt[:, None, :, :]).reshape(width_all)
    pair_sums = jnp.dot(fitted.T, fitted, preferred_element_type=jnp.float32)
    pattern_now = lax.dynamic_index_in_dim(pair_pattern, group, 0, keepdims=False).astype(jnp.float32)
    width_block = width_all // block_count
    mask_full = jnp.repeat(jnp.repeat(pattern_now, width_block, axis=0), width_block, axis=1)
    amplitudes = (mask_full * pair_sums / (col_energy[:, None] + col_energy[None, :])).astype(jnp.bfloat16)
    return jnp.dot(fitted, amplitudes.T, preferred_element_type=jnp.float32).astype(jnp.bfloat16)


def reference(integrals, domain_transforms, domain_lists, occ_energies, virt_energies, pair_pattern):
    def per_group(group):
        return one_group(integrals, domain_transforms, domain_lists, occ_energies, virt_energies, pair_pattern, group)

    stacked = lax.map(per_group, jnp.arange(NGRP, dtype=jnp.int32))
    return jnp.moveaxis(stacked, 0, 1)
```

```python
import functools

import jax
import jax.numpy as jnp
from jax import lax
from jax.experimental import pallas as pl
from jax.experimental.pallas import tpu as pltpu
from jax.sharding import PartitionSpec as P

VB = 24
NDOM = 5
OB = 1
LANES = 128
F32 = jnp.float32
BF16 = jnp.bfloat16
NT = (((1,), (1,)), ((), ()))


def tile_iota(size):
    row = lax.broadcasted_iota(jnp.int32, (size, size), 0)
    col = lax.broadcasted_iota(jnp.int32, (size, size), 1)
    return row, col


def fit_kernel(half, lists_ref, trans_ref, raw_ref, fit_ref, part_ref, wide_ref):
    width = raw_ref.shape[1]
    pad = fit_ref.shape[1] // 2
    blocks = width // VB
    group = pl.program_id(0)

    @pl.when(group == 0)
    def _():
        row = lax.broadcasted_iota(jnp.int32, (VB, width), 0)
        col = lax.broadcasted_iota(jnp.int32, (VB, width), 1)
        spread = (lax.rem(col, VB) == row).astype(BF16)
        wide = jnp.dot(trans_ref[...], spread, preferred_element_type=F32)
        wide_ref[...] = wide.reshape(wide_ref.shape)

    lane_block = lax.div(lax.broadcasted_iota(jnp.int32, (VB, width), 1), VB)
    rows = []
    for block in range(blocks):
        which = lists_ref[group * blocks + block]
        rows.append(jnp.where(lane_block == block, wide_ref[which], 0.0))
        if (block + 1) * 2 % blocks == 0:
            rows.append(jnp.zeros((pad - half, width), F32))
    mixer = jnp.concatenate(rows, axis=0).astype(BF16)
    fit = jnp.dot(mixer, raw_ref[0], preferred_element_type=F32).astype(BF16)
    fit_ref[0] = fit
    sums = lax.dot_general(fit, fit, NT, preferred_element_type=F32)
    row, col = tile_iota(pad)
    first, last, cross = sums[:pad, :pad], sums[pad:, pad:], sums[:pad, pad:]
    diag = jnp.sum(jnp.where(row == col, last, 0.0), axis=1, keepdims=True)
    packed = jnp.where(row >= col, first, last)
    packed = jnp.where(col == half, diag, packed)
    part_ref[0, 0] = packed.astype(part_ref.dtype)
    part_ref[1, 0] = cross.astype(part_ref.dtype)


def fit_call(raw, transforms, lists, half, pad):
    groups, width, aux = raw.shape
    count = transforms.shape[0]
    flat = jnp.swapaxes(transforms, 1, 2).reshape(count * VB, VB)
    return pl.pallas_call(
        functools.partial(fit_kernel, half),
        grid_spec=pltpu.PrefetchScalarGridSpec(
            num_scalar_prefetch=1,
            grid=(groups,),
            in_specs=[
                pl.BlockSpec((count * VB, VB), lambda g, s: (0, 0)),
                pl.BlockSpec((1, width, aux), lambda g, s: (g, 0, 0)),
            ],
            out_specs=[
                pl.BlockSpec((1, 2 * pad, aux), lambda g, s: (g, 0, 0)),
                pl.BlockSpec((2, 1, pad, pad), lambda g, s: (0, g, 0, 0)),
            ],
            scratch_shapes=[pltpu.VMEM((count, VB, width), F32)],
        ),
        out_shape=[
            jax.ShapeDtypeStruct((groups, 2 * pad, aux), BF16),
            jax.ShapeDtypeStruct((2, groups, pad, pad), BF16),
        ],
        name="fit",
    )(lists.reshape(-1), flat, raw)


def gamma_kernel(half, amp_ref, fit_ref, out_ref):
    pad = fit_ref.shape[1] // 2
    packed = amp_ref[0, 0].astype(F32)
    cross = amp_ref[1, 0].astype(F32)
    row, col = tile_iota(pad)
    flipped = packed.T
    diag = packed[:, half : half + 1]
    first = jnp.where(row >= col, packed, flipped)
    last = jnp.where(row < col, packed, jnp.where(row == col, diag, flipped))
    top = jnp.concatenate([first, cross], axis=1)[:half]
    bottom = jnp.concatenate([cross.T, last], axis=1)[:half]
    amp = jnp.concatenate([top, bottom], axis=0).astype(BF16)
    out_ref[0] = jnp.dot(amp, fit_ref[0], preferred_element_type=F32).astype(BF16)


def gamma_call(amps, fit, half):
    groups, double, aux = fit.shape
    pad = double // 2
    return pl.pallas_call(
        functools.partial(gamma_kernel, half),
        grid=(groups,),
        in_specs=[
            pl.BlockSpec((2, 1, pad, pad), lambda g: (0, g, 0, 0)),
            pl.BlockSpec((1, double, aux), lambda g: (g, 0, 0)),
        ],
        out_specs=pl.BlockSpec((1, 2 * half, aux), lambda g: (g, 0, 0)),
        out_shape=jax.ShapeDtypeStruct((groups, 2 * half, aux), BF16),
        name="gamma",
    )(amps, fit)


def pair_scale(core, half, row_e, col_e, pattern):
    size = row_e.shape[1]
    row, col = tile_iota(size)
    first = pattern[0] / (col_e[:, 0:1] + row_e[0:1, :])
    last = pattern[3] / (col_e[:, 1:2] + row_e[1:2, :])
    cross = pattern[1] / (col_e[:, 0:1] + row_e[1:2, :])
    packed = jnp.where(row >= col, first, last)
    packed = jnp.where(col == half, pattern[3] / (2.0 * col_e[:, 1:2]), packed)
    return jnp.where(core == 0, packed, cross)


def exchange_kernel(half, nz, pattern_ref, row_ref, col_ref, part_ref, out_ref,
                    got_core, sum_core, got_x, sum_x, got_y, sum_y, got_z, send_sem, recv_sem):
    core = lax.axis_index("blk")
    here = lax.axis_index("occ")
    x = lax.rem(here, 2)
    y = lax.rem(lax.div(here, 2), 2)
    z = lax.div(here, 4)
    other_core = (here, 1 - core)
    other_x = (here + 1 - 2 * x, core)
    other_y = (here + 2 - 4 * y, core)
    others_z = [(lax.rem(z + d, nz) * 4 + y * 2 + x, core) for d in range(1, nz)]

    barrier = pltpu.get_barrier_semaphore()
    peers = [other_core, other_x, other_y] + others_z
    for peer in peers:
        pl.semaphore_signal(barrier, inc=1, device_id=peer, device_id_type=pl.DeviceIdType.MESH)
    pl.semaphore_wait(barrier, len(peers))

    def copy(slot, source, target, peer):
        return pltpu.make_async_remote_copy(
            src_ref=source, dst_ref=target, send_sem=send_sem.at[slot],
            recv_sem=recv_sem.at[slot], device_id=peer,
            device_id_type=pl.DeviceIdType.MESH,
        )

    def add(target, left, right):
        target[...] = (left.astype(F32) + right.astype(F32)).astype(BF16)

    move = copy(0, part_ref.at[1 - core], got_core, other_core)
    move.start()
    scale = pair_scale(core, half, row_ref[...], col_ref[...], [pattern_ref[i] for i in range(4)])
    move.wait()
    add(sum_core, part_ref[core], got_core[...])
    move = copy(1, sum_core.at[:, :, 1 - x], got_x, other_x)
    move.start()
    move.wait()
    add(sum_x, sum_core[:, :, x], got_x[...])
    move = copy(2, sum_x.at[:, 1 - y], got_y, other_y)
    move.start()
    move.wait()
    add(sum_y, sum_x[:, y], got_y[...])
    moves = []
    for d in range(1, nz):
        move = copy(2 + d, sum_y.at[lax.rem(z + d, nz)], got_z.at[d - 1], others_z[d - 1])
        move.start()
        moves.append(move)
    total = sum_y[z].astype(F32)
    for d, move in enumerate(moves):
        move.wait()
        total += got_z[d].astype(F32)
    out_ref[core, z, y, x] = (total * scale).astype(BF16)
    moves = []
    base = 2 + nz
    for d in range(1, nz):
        spot = out_ref.at[core, z, y, x]
        move = copy(base + d - 1, spot, spot, others_z[d - 1])
        move.start()
        moves.append(move)
    for move in moves:
        move.wait()
    base += nz - 1
    spot = out_ref.at[core, :, y, x]
    move = copy(base, spot, spot, other_y)
    move.start()
    move.wait()
    spot = out_ref.at[core, :, :, x]
    move = copy(base + 1, spot, spot, other_x)
    move.start()
    move.wait()
    spot = out_ref.at[core]
    move = copy(base + 2, spot, spot, other_core)
    move.start()
    move.wait()


def exchange_call(parts, row_e, col_e, pattern, half):
    _, groups, pad, _ = parts.shape
    nz = groups // 4
    tile = (pad, pad)
    parts = parts.reshape((2, nz, 2, 2) + tile)
    vmem = pl.BlockSpec(memory_space=pltpu.VMEM)
    slots = 3 + (nz - 1) * 2 + 3
    amps = pl.pallas_call(
        functools.partial(exchange_kernel, half, nz),
        in_specs=[pl.BlockSpec(memory_space=pltpu.SMEM), vmem, vmem, vmem],
        out_specs=vmem,
        out_shape=jax.ShapeDtypeStruct((2, nz, 2, 2) + tile, BF16),
        scratch_shapes=[
            pltpu.VMEM((nz, 2, 2) + tile, BF16),
            pltpu.VMEM((nz, 2, 2) + tile, BF16),
            pltpu.VMEM((nz, 2) + tile, BF16),
            pltpu.VMEM((nz, 2) + tile, BF16),
            pltpu.VMEM((nz,) + tile, BF16),
            pltpu.VMEM((nz,) + tile, BF16),
            pltpu.VMEM((nz - 1,) + tile, BF16),
            pltpu.SemaphoreType.DMA((slots,)),
            pltpu.SemaphoreType.DMA((slots,)),
        ],
        compiler_params=pltpu.CompilerParams(collective_id=0, has_side_effects=True),
        name="exchange",
    )(pattern, row_e, col_e, parts)
    return amps.reshape((2, groups) + tile)


def build_fitted(raw_rows, transforms):
    row_count, group_count, width_all = raw_rows.shape
    block_count = transforms.shape[1]
    shaped = raw_rows.reshape(row_count, group_count, block_count, OB, NDOM, VB)
    mixed = jnp.einsum(
        "pgbomu,gbmuv->pgbomv", shaped, transforms, preferred_element_type=jnp.float32
    )
    return mixed.astype(jnp.bfloat16).reshape(row_count, group_count, width_all)


def on_device(
    integrals, domain_transforms, domain_lists, occ_energies, virt_energies, pair_pattern
):
    group_here = lax.axis_index("occ")
    own_lists = lax.dynamic_index_in_dim(domain_lists, group_here, 0, keepdims=True)
    every_transform = jnp.take(domain_transforms, domain_lists, axis=0)
    fitted_all = build_fitted(integrals, every_transform)
    fitted = lax.all_to_all(fitted_all, "occ", split_axis=1, concat_axis=0, tiled=True)
    aux_rows = fitted.shape[0]
    width_all = fitted.shape[2]
    fitted = fitted.reshape(aux_rows, width_all)
    block_count = pair_pattern.shape[1]
    width_block = width_all // block_count
    block_virt = jnp.take(virt_energies, own_lists[0], axis=0)
    col_energy = (occ_energies[0][:, :, None, None] - block_virt[:, None, :, :]).reshape(width_all)
    pattern_now = pair_pattern[0]
    pattern_float = pattern_now.astype(jnp.float32)
    mask_full = jnp.repeat(jnp.repeat(pattern_float, width_block, axis=0), width_block, axis=1)
    partial_sums = lax.dot_general(
        fitted, fitted, (((0,), (0,)), ((), ())), preferred_element_type=jnp.float32
    )
    row_sums = lax.psum_scatter(partial_sums, "blk", scatter_dimension=0, tiled=True)
    share_rows = row_sums.shape[0]
    block_here = lax.axis_index("blk")
    row_energy = lax.dynamic_slice_in_dim(col_energy, block_here * share_rows, share_rows, 0)
    row_mask = lax.dynamic_slice_in_dim(mask_full, block_here * share_rows, share_rows, 0)
    row_amplitudes = (row_mask * row_sums / (row_energy[:, None] + col_energy[None, :])).astype(
        jnp.bfloat16
    )
    amplitudes = lax.all_gather(row_amplitudes, "blk", axis=0, tiled=True)
    gamma_rows = lax.dot_general(
        fitted, amplitudes, (((1,), (1,)), ((), ())), preferred_element_type=jnp.float32
    )
    gamma_rows = gamma_rows.astype(jnp.bfloat16).reshape(aux_rows, 1, width_all)
    return lax.all_to_all(gamma_rows, "occ", split_axis=0, concat_axis=1, tiled=True)


def local_sums(
    integrals, domain_transforms, domain_lists, occ_energies, virt_energies, pair_pattern
):
    width = integrals.shape[2]
    half = width // 2
    pad = -(-half // LANES) * LANES
    group_here = lax.axis_index("occ")
    own_lists = lax.dynamic_index_in_dim(domain_lists, group_here, 0, keepdims=False)
    block_virt = jnp.take(virt_energies, own_lists, axis=0)
    energy = (occ_energies[0][:, :, None, None] - block_virt[:, None, :, :]).reshape(2, half)
    row_e = jnp.pad(energy, ((0, 0), (0, pad - half)), constant_values=-1.0)
    pattern = pair_pattern[0].astype(F32).reshape(4)
    fit, parts = fit_call(
        jnp.transpose(integrals, (1, 2, 0)), domain_transforms, domain_lists, half, pad
    )
    amps = exchange_call(parts, row_e, row_e.T, pattern, half)
    return jnp.transpose(gamma_call(amps, fit, half), (2, 0, 1))


def sums_are_smaller(mesh, integrals, pair_pattern):
    rows = integrals.shape[0] // mesh.size
    groups, width = integrals.shape[1:]
    half = width // 2
    return (
        width <= rows
        and rows % LANES == 0
        and pair_pattern.shape[1] == 2
        and mesh.shape["blk"] == 2
        and mesh.shape["occ"] == groups
        and groups % 4 == 0
        and groups >= 8
        and half % VB == 0
        and half % LANES != 0
        and half < LANES
    )


def solution(mesh):
    def program(*args):
        body = local_sums if sums_are_smaller(mesh, args[0], args[5]) else on_device
        return jax.shard_map(
            body,
            mesh=mesh,
            in_specs=(
                P(("occ", "blk"), None, None),
                P(),
                P(),
                P("occ", None, None),
                P(),
                P("occ", None, None),
            ),
            out_specs=P(("occ", "blk"), None, None),
            check_vma=False,
        )(*args)

    return program
```

```python
import functools

import jax
import jax.numpy as jnp
from jax import lax
from jax.experimental import pallas as pl
from jax.experimental.pallas import tpu as pltpu
from jax.sharding import PartitionSpec as P

VB = 24
NDOM = 5
OB = 1
LANES = 128
F32 = jnp.float32
BF16 = jnp.bfloat16
NT = (((1,), (1,)), ((), ()))


def tile_iota(size):
    row = lax.broadcasted_iota(jnp.int32, (size, size), 0)
    col = lax.broadcasted_iota(jnp.int32, (size, size), 1)
    return row, col


def pair_kernel(half, nz, lists_ref, pattern_ref, occ_ref, virt_ref, trans_ref, raw_ref,
                amp_ref, fit_out, wide_ref, raw_buf, fit_buf, parts, got_core, sum_core,
                got_x, sum_x, got_y, sum_y, got_z, in_sem, out_sem, send_sem, recv_sem):
    core = lax.axis_index("blk")
    here = lax.axis_index("occ")
    x = lax.rem(here, 2)
    y = lax.rem(lax.div(here, 2), 2)
    z = lax.div(here, 4)
    at_core = (here, 1 - core)
    at_x = (here + 1 - 2 * x, core)
    at_y = (here + 2 - 4 * y, core)

    def plane(d):
        return lax.rem(z + d, nz)

    def at_z(d):
        return (plane(d) * 4 + y * 2 + x, core)

    steps = 2 * nz
    width = raw_ref.shape[3]
    pad = parts.shape[-1]
    blocks = width // VB

    def place(s):
        return plane(s // 2 + 1), lax.rem(y + 1 + s % 2, 2)

    loads = []
    for s in range(steps):
        zr, yr = place(s)
        loads.append(pltpu.make_async_copy(raw_ref.at[zr, yr], raw_buf.at[s], in_sem.at[s]))
        loads[-1].start()

    barrier = pltpu.get_barrier_semaphore()
    peers = [at_core, at_x, at_y] + [at_z(d) for d in range(1, nz)]
    for peer in peers:
        pl.semaphore_signal(barrier, inc=1, device_id=peer, device_id_type=pl.DeviceIdType.MESH)

    spread_row = lax.broadcasted_iota(jnp.int32, (VB, width), 0)
    spread_col = lax.broadcasted_iota(jnp.int32, (VB, width), 1)
    spread = (lax.rem(spread_col, VB) == spread_row).astype(BF16)
    wide = jnp.dot(trans_ref[...], spread, preferred_element_type=F32)
    wide_ref[...] = wide.reshape(wide_ref.shape)
    lane_block = lax.div(spread_col, VB)
    row, col = tile_iota(pad)

    virt = virt_ref[...]
    domain = lax.broadcasted_iota(jnp.int32, virt.shape, 1)
    columns = []
    for h in range(2):
        pieces = []
        for j in range(blocks // 2):
            which = lists_ref[j, h, here]
            energy = jnp.sum(jnp.where(domain == which, virt, 0.0), axis=1, keepdims=True)
            pieces.append(occ_ref[h] - energy)
        pieces.append(jnp.full((pad - half, 1), -1.0, F32))
        columns.append(jnp.broadcast_to(jnp.concatenate(pieces, axis=0), (pad, pad)))
    keep = [pattern_ref[i, j].astype(F32) for i, j in ((0, 0), (0, 1), (1, 1))]
    flip = columns[1].T
    scale = jnp.where(row >= col, keep[0] / (columns[0] + columns[0].T),
                      keep[2] / (columns[1] + flip))
    scale = jnp.where(col == half, keep[2] / (columns[1] + columns[1]), scale)
    scale = jnp.where(core == 0, scale, keep[1] / (columns[0] + flip))

    pl.semaphore_wait(barrier, len(peers))

    sent = []
    slots = iter(range(10**6))

    def copy(source, target, peer):
        slot = next(slots)
        move = pltpu.make_async_remote_copy(
            src_ref=source, dst_ref=target, send_sem=send_sem.at[slot],
            recv_sem=recv_sem.at[slot], device_id=peer,
            device_id_type=pl.DeviceIdType.MESH,
        )
        move.start()
        sent.append(move)
        return move

    def compute(s):
        loads[s].wait()
        zr, yr = place(s)
        for side in range(2):
            group = zr * 4 + yr * 2 + side
            rows = []
            for block in range(blocks):
                h, j = divmod(block, blocks // 2)
                which = lists_ref[j, h, group]
                rows.append(jnp.where(lane_block == block, wide_ref[which], 0.0))
                if (block + 1) * 2 % blocks == 0:
                    rows.append(jnp.zeros((pad - half, width), F32))
            mixer = jnp.concatenate(rows, axis=0).astype(BF16)
            fit = jnp.dot(mixer, raw_buf[s, side], preferred_element_type=F32).astype(BF16)
            fit_buf[s, side] = fit
            sums = lax.dot_general(fit, fit, NT, preferred_element_type=F32)
            first, last = sums[:pad, :pad], sums[pad:, pad:]
            diag = jnp.sum(jnp.where(row == col, last, 0.0), axis=1, keepdims=True)
            packed = jnp.where(row >= col, first, last)
            parts[0, s, side] = jnp.where(col == half, diag, packed).astype(BF16)
            parts[1, s, side] = sums[:pad, pad:].astype(BF16)
        store = pltpu.make_async_copy(fit_buf.at[s], fit_out.at[zr, yr], out_sem.at[s])
        store.start()
        return store

    def add(left, right):
        return (left.astype(F32) + right.astype(F32)).astype(BF16)

    stores, by_core, by_x, by_y, by_z = [], {}, {}, {}, {}
    for t in range(steps + 5):
        if t < steps:
            stores.append(compute(t))
            by_core[t] = copy(parts.at[1 - core, t], got_core.at[t], at_core)
        s = t - 1
        if 0 <= s < steps:
            by_core[s].wait_recv()
            sum_core[s] = add(parts[core, s], got_core[s])
            by_x[s] = copy(sum_core.at[s, 1 - x], got_x.at[s], at_x)
        s = t - 3
        if 0 <= s < steps:
            by_x[s].wait_recv()
            sum_x[s] = add(sum_core[s, x], got_x[s])
            if s % 2 == 0:
                by_y[s // 2] = copy(sum_x.at[s], got_y.at[s // 2], at_y)
        s = t - 5
        if 0 <= s < steps and s % 2 == 1:
            d = s // 2
            by_y[d].wait_recv()
            sum_y[d] = add(sum_x[s], got_y[d])
            if d < nz - 1:
                by_z[d] = copy(sum_y.at[d], got_z.at[d], at_z(d + 1))
    total = sum_y[nz - 1].astype(F32)
    for d in range(nz - 1):
        by_z[d].wait_recv()
        total += got_z[d].astype(F32)
    amp_ref[core, z, y, x] = (total * scale).astype(BF16)

    def tile(d, yr, xr):
        return amp_ref.at[core, plane(d), yr, xr]

    def pass_on(d, yr, xr, peer):
        return copy(tile(d, yr, xr), tile(d, yr, xr), peer)

    def fan_out(d):
        if d == 0:
            for e in range(1, nz):
                from_z[nz - e] = pass_on(0, y, x, at_z(e))
        else:
            from_z[d].wait_recv()
        from_y[d] = pass_on(d, y, x, at_y)
        from_x[d] = pass_on(d, y, x, at_x)
        from_core.append(pass_on(d, y, x, at_core))

    def cross_over(d):
        from_y[d].wait_recv()
        if d % 2 == 0:
            from_corner[d] = pass_on(d, 1 - y, x, at_x)
        from_core.append(pass_on(d, 1 - y, x, at_core))
        from_x[d].wait_recv()
        if d % 2 == 1:
            from_corner[d] = pass_on(d, y, 1 - x, at_y)
        from_core.append(pass_on(d, y, 1 - x, at_core))

    from_z, from_y, from_x, from_corner, from_core = {}, {}, {}, {}, []
    order = [0] + sorted(range(1, nz), key=lambda d: (min(d, nz - d), d))
    for i, d in enumerate(order):
        fan_out(d)
        if i >= 1:
            cross_over(order[i - 1])
    cross_over(order[-1])
    for d in order:
        from_corner[d].wait_recv()
        from_core.append(pass_on(d, 1 - y, 1 - x, at_core))
    for move in from_core:
        move.wait_recv()
    for move in sent:
        move.wait_send()
    for store in stores:
        store.wait()


def pair_call(raw, transforms, lists, occ, virt, pattern, half, pad):
    groups, width, aux = raw.shape
    nz = groups // 4
    steps = 2 * nz
    count = transforms.shape[0]
    tile = (pad, pad)
    flat = jnp.swapaxes(transforms, 1, 2).reshape(count * VB, VB)
    vmem = pl.BlockSpec(memory_space=pltpu.VMEM)
    smem = pl.BlockSpec(memory_space=pltpu.SMEM)
    hbm = pl.BlockSpec(memory_space=pl.ANY)
    slots = 2 * steps + nz + (nz - 1) + (nz - 1) + nz * 8
    amps, fit = pl.pallas_call(
        functools.partial(pair_kernel, half, nz),
        in_specs=[smem, smem, smem, vmem, vmem, hbm],
        out_specs=[vmem, hbm],
        out_shape=[
            jax.ShapeDtypeStruct((2, nz, 2, 2) + tile, BF16),
            jax.ShapeDtypeStruct((nz, 2, 2, 2 * pad, aux), BF16),
        ],
        scratch_shapes=[
            pltpu.VMEM((count, VB, width), F32),
            pltpu.VMEM((steps, 2, width, aux), BF16),
            pltpu.VMEM((steps, 2, 2 * pad, aux), BF16),
            pltpu.VMEM((2, steps, 2) + tile, BF16),
            pltpu.VMEM((steps, 2) + tile, BF16),
            pltpu.VMEM((steps, 2) + tile, BF16),
            pltpu.VMEM((steps,) + tile, BF16),
            pltpu.VMEM((steps,) + tile, BF16),
            pltpu.VMEM((nz,) + tile, BF16),
            pltpu.VMEM((nz,) + tile, BF16),
            pltpu.VMEM((nz - 1,) + tile, BF16),
            pltpu.SemaphoreType.DMA((steps,)),
            pltpu.SemaphoreType.DMA((steps,)),
            pltpu.SemaphoreType.DMA((slots,)),
            pltpu.SemaphoreType.DMA((slots,)),
        ],
        compiler_params=pltpu.CompilerParams(collective_id=0, has_side_effects=True),
        name="pairs",
    )(
        jnp.transpose(lists, (2, 1, 0)), pattern, occ, virt.T, flat,
        raw.reshape(nz, 2, 2, width, aux),
    )
    return amps.reshape((2, groups) + tile), fit.reshape(groups, 2 * pad, aux)


def gamma_kernel(half, amp_ref, fit_ref, out_ref):
    pad = fit_ref.shape[1] // 2
    row, col = tile_iota(pad)
    for i in range(fit_ref.shape[0]):
        packed = amp_ref[0, i].astype(F32)
        cross = amp_ref[1, i].astype(F32)
        flipped = packed.T
        diag = packed[:, half : half + 1]
        first = jnp.where(row >= col, packed, flipped)
        last = jnp.where(row < col, packed, jnp.where(row == col, diag, flipped))
        top = jnp.concatenate([first, cross], axis=1)[:half]
        bottom = jnp.concatenate([cross.T, last], axis=1)[:half]
        amp = jnp.concatenate([top, bottom], axis=0).astype(BF16)
        out_ref[i] = jnp.dot(amp, fit_ref[i], preferred_element_type=F32).astype(BF16)


def gamma_call(amps, fit, half):
    groups, double, aux = fit.shape
    pad = double // 2
    some = 2
    return pl.pallas_call(
        functools.partial(gamma_kernel, half),
        grid=(groups // some,),
        in_specs=[
            pl.BlockSpec((2, some, pad, pad), lambda g: (0, g, 0, 0)),
            pl.BlockSpec((some, double, aux), lambda g: (g, 0, 0)),
        ],
        out_specs=pl.BlockSpec((some, 2 * half, aux), lambda g: (g, 0, 0)),
        out_shape=jax.ShapeDtypeStruct((groups, 2 * half, aux), BF16),
        name="gamma",
    )(amps, fit)


def build_fitted(raw_rows, transforms):
    row_count, group_count, width_all = raw_rows.shape
    block_count = transforms.shape[1]
    shaped = raw_rows.reshape(row_count, group_count, block_count, OB, NDOM, VB)
    mixed = jnp.einsum(
        "pgbomu,gbmuv->pgbomv", shaped, transforms, preferred_element_type=jnp.float32
    )
    return mixed.astype(jnp.bfloat16).reshape(row_count, group_count, width_all)


def on_device(
    integrals, domain_transforms, domain_lists, occ_energies, virt_energies, pair_pattern
):
    group_here = lax.axis_index("occ")
    own_lists = lax.dynamic_index_in_dim(domain_lists, group_here, 0, keepdims=True)
    every_transform = jnp.take(domain_transforms, domain_lists, axis=0)
    fitted_all = build_fitted(integrals, every_transform)
    fitted = lax.all_to_all(fitted_all, "occ", split_axis=1, concat_axis=0, tiled=True)
    aux_rows = fitted.shape[0]
    width_all = fitted.shape[2]
    fitted = fitted.reshape(aux_rows, width_all)
    block_count = pair_pattern.shape[1]
    width_block = width_all // block_count
    block_virt = jnp.take(virt_energies, own_lists[0], axis=0)
    col_energy = (occ_energies[0][:, :, None, None] - block_virt[:, None, :, :]).reshape(width_all)
    pattern_now = pair_pattern[0]
    pattern_float = pattern_now.astype(jnp.float32)
    mask_full = jnp.repeat(jnp.repeat(pattern_float, width_block, axis=0), width_block, axis=1)
    partial_sums = lax.dot_general(
        fitted, fitted, (((0,), (0,)), ((), ())), preferred_element_type=jnp.float32
    )
    row_sums = lax.psum_scatter(partial_sums, "blk", scatter_dimension=0, tiled=True)
    share_rows = row_sums.shape[0]
    block_here = lax.axis_index("blk")
    row_energy = lax.dynamic_slice_in_dim(col_energy, block_here * share_rows, share_rows, 0)
    row_mask = lax.dynamic_slice_in_dim(mask_full, block_here * share_rows, share_rows, 0)
    row_amplitudes = (row_mask * row_sums / (row_energy[:, None] + col_energy[None, :])).astype(
        jnp.bfloat16
    )
    amplitudes = lax.all_gather(row_amplitudes, "blk", axis=0, tiled=True)
    gamma_rows = lax.dot_general(
        fitted, amplitudes, (((1,), (1,)), ((), ())), preferred_element_type=jnp.float32
    )
    gamma_rows = gamma_rows.astype(jnp.bfloat16).reshape(aux_rows, 1, width_all)
    return lax.all_to_all(gamma_rows, "occ", split_axis=0, concat_axis=1, tiled=True)


def local_sums(
    integrals, domain_transforms, domain_lists, occ_energies, virt_energies, pair_pattern
):
    width = integrals.shape[2]
    half = width // 2
    pad = -(-half // LANES) * LANES
    amps, fit = pair_call(
        jnp.transpose(integrals, (1, 2, 0)), domain_transforms, domain_lists,
        occ_energies.reshape(2), virt_energies, pair_pattern[0], half, pad,
    )
    return jnp.transpose(gamma_call(amps, fit, half), (2, 0, 1))


def sums_are_smaller(mesh, integrals, pair_pattern):
    rows = integrals.shape[0] // mesh.size
    groups, width = integrals.shape[1:]
    half = width // 2
    return (
        width <= rows
        and rows % LANES == 0
        and pair_pattern.shape[1] == 2
        and mesh.shape["blk"] == 2
        and mesh.shape["occ"] == groups
        and groups % 4 == 0
        and groups >= 8
        and half % VB == 0
        and half % LANES != 0
        and half < LANES
    )


def solution(mesh):
    def program(*args):
        body = local_sums if sums_are_smaller(mesh, args[0], args[5]) else on_device
        return jax.shard_map(
            body,
            mesh=mesh,
            in_specs=(
                P(("occ", "blk"), None, None),
                P(),
                P(),
                P("occ", None, None),
                P(),
                P("occ", None, None),
            ),
            out_specs=P(("occ", "blk"), None, None),
            check_vma=False,
        )(*args)

    return program
```

```python
import functools

import jax
import jax.numpy as jnp
from jax import lax
from jax.experimental import pallas as pl
from jax.experimental.pallas import tpu as pltpu
from jax.sharding import PartitionSpec as P

VB = 24
NDOM = 5
OB = 1
LANES = 128
F32 = jnp.float32
BF16 = jnp.bfloat16
NT = (((1,), (1,)), ((), ()))


def tile_iota(size):
    row = lax.broadcasted_iota(jnp.int32, (size, size), 0)
    col = lax.broadcasted_iota(jnp.int32, (size, size), 1)
    return row, col


def pair_kernel(half, nz, lists_ref, pattern_ref, occ_ref, virt_ref, trans_ref, raw_ref,
                amp_ref, fit_out, wide_ref, raw_buf, fit_buf, parts, got_core, sum_core,
                got_x, sum_x, got_y, sum_y, got_z, in_sem, out_sem, send_sem, recv_sem):
    core = lax.axis_index("blk")
    here = lax.axis_index("occ")
    x = lax.rem(here, 2)
    y = lax.rem(lax.div(here, 2), 2)
    z = lax.div(here, 4)
    at_core = (here, 1 - core)
    at_x = (here + 1 - 2 * x, core)
    at_y = (here + 2 - 4 * y, core)

    def plane(d):
        return lax.rem(z + d, nz)

    def at_z(d):
        return (plane(d) * 4 + y * 2 + x, core)

    steps = 2 * nz
    width = raw_ref.shape[3]
    pad = parts.shape[-1]
    blocks = width // VB

    def place(s):
        return plane(s // 2 + 1), lax.rem(y + 1 + s % 2, 2)

    loads = []
    for s in range(steps):
        zr, yr = place(s)
        loads.append(pltpu.make_async_copy(raw_ref.at[zr, yr], raw_buf.at[s], in_sem.at[s]))
        loads[-1].start()

    barrier = pltpu.get_barrier_semaphore()
    peers = [at_core, at_x, at_y] + [at_z(d) for d in range(1, nz)]
    for peer in peers:
        pl.semaphore_signal(barrier, inc=1, device_id=peer, device_id_type=pl.DeviceIdType.MESH)

    spread_row = lax.broadcasted_iota(jnp.int32, (VB, width), 0)
    spread_col = lax.broadcasted_iota(jnp.int32, (VB, width), 1)
    spread = (lax.rem(spread_col, VB) == spread_row).astype(BF16)
    wide = jnp.dot(trans_ref[...], spread, preferred_element_type=F32)
    wide_ref[...] = wide.reshape(wide_ref.shape)
    lane_block = lax.div(spread_col, VB)
    row, col = tile_iota(pad)

    def pair_scale():
        virt = virt_ref[...]
        domain = lax.broadcasted_iota(jnp.int32, virt.shape, 1)
        columns = []
        for h in range(2):
            pieces = []
            for j in range(blocks // 2):
                which = lists_ref[j, h, here]
                energy = jnp.sum(jnp.where(domain == which, virt, 0.0), axis=1, keepdims=True)
                pieces.append(occ_ref[h] - energy)
            pieces.append(jnp.full((pad - half, 1), -1.0, F32))
            columns.append(jnp.broadcast_to(jnp.concatenate(pieces, axis=0), (pad, pad)))
        keep = [pattern_ref[i, j].astype(F32) for i, j in ((0, 0), (0, 1), (1, 1))]
        flip = columns[1].T
        scale = jnp.where(row >= col, keep[0] / (columns[0] + columns[0].T),
                          keep[2] / (columns[1] + flip))
        scale = jnp.where(col == half, keep[2] / (columns[1] + columns[1]), scale)
        return jnp.where(core == 0, scale, keep[1] / (columns[0] + flip))

    sent = []
    slots = iter(range(10**6))

    def copy(source, target, peer):
        slot = next(slots)
        move = pltpu.make_async_remote_copy(
            src_ref=source, dst_ref=target, send_sem=send_sem.at[slot],
            recv_sem=recv_sem.at[slot], device_id=peer,
            device_id_type=pl.DeviceIdType.MESH,
        )
        move.start()
        sent.append(move)
        return move

    def compute(s):
        loads[s].wait()
        zr, yr = place(s)
        for side in range(2):
            group = zr * 4 + yr * 2 + side
            rows = []
            for block in range(blocks):
                h, j = divmod(block, blocks // 2)
                which = lists_ref[j, h, group]
                rows.append(jnp.where(lane_block == block, wide_ref[which], 0.0))
                if (block + 1) * 2 % blocks == 0:
                    rows.append(jnp.zeros((pad - half, width), F32))
            mixer = jnp.concatenate(rows, axis=0).astype(BF16)
            fit = jnp.dot(mixer, raw_buf[s, side], preferred_element_type=F32).astype(BF16)
            fit_buf[s, side] = fit
            sums = lax.dot_general(fit, fit, NT, preferred_element_type=F32)
            first, last = sums[:pad, :pad], sums[pad:, pad:]
            diag = jnp.sum(jnp.where(row == col, last, 0.0), axis=1, keepdims=True)
            packed = jnp.where(row >= col, first, last)
            parts[0, s, side] = jnp.where(col == half, diag, packed).astype(BF16)
            parts[1, s, side] = sums[:pad, pad:].astype(BF16)
        store = pltpu.make_async_copy(fit_buf.at[s], fit_out.at[zr, yr], out_sem.at[s])
        store.start()
        return store

    def add(left, right):
        return (left.astype(F32) + right.astype(F32)).astype(BF16)

    stores, by_core, by_x, by_y, by_z = [], {}, {}, {}, {}
    for t in range(steps + 4):
        if t < steps:
            stores.append(compute(t))
            if t == 0:
                pl.semaphore_wait(barrier, len(peers))
            by_core[t] = copy(parts.at[1 - core, t], got_core.at[t], at_core)
        elif t == steps:
            scale = pair_scale()
        s = t - 1
        if 0 <= s < steps:
            by_core[s].wait_recv()
            sum_core[s] = add(parts[core, s], got_core[s])
            by_x[s] = copy(sum_core.at[s, 1 - x], got_x.at[s], at_x)
        s = t - 4
        if 0 <= s < steps and s % 2 == 1 and t != steps + 3:
            d = s // 2
            by_y[d].wait_recv()
            sum_y[d] = add(sum_x[s], got_y[d])
            by_z[d] = copy(sum_y.at[d], got_z.at[d], at_z(d + 1))
        s = t - 3
        if 0 <= s < steps:
            by_x[s].wait_recv()
            sum_x[s] = add(sum_core[s, x], got_x[s])
            if s % 2 == 0:
                by_y[s // 2] = copy(sum_x.at[s], got_y.at[s // 2], at_y)
    by_y[nz - 1].wait_recv()
    sum_y[nz - 1] = add(sum_x[steps - 1], got_y[nz - 1])
    total = sum_y[nz - 1].astype(F32)
    for d in range(nz - 1):
        by_z[d].wait_recv()
        total += got_z[d].astype(F32)
    amp_ref[core, z, y, x] = (total * scale).astype(BF16)

    near = [z]
    low, high = z - 1, z + 1
    for i in range(1, nz):
        rise = jnp.logical_and(high < nz, jnp.logical_or(low < 0, high - z <= z - low))
        near.append(jnp.where(rise, high, low))
        low = jnp.where(rise, low, low - 1)
        high = jnp.where(rise, high + 1, high)

    def pass_on(plane, yr, xr, peer):
        spot = amp_ref.at[core, plane, yr, xr]
        return copy(spot, spot, peer)

    def fan_out(i):
        if i == 0:
            for e in range(nz - 1, 0, -1):
                spot = amp_ref.at[core, z, y, x]
                move = pltpu.make_async_remote_copy(
                    src_ref=spot, dst_ref=spot, send_sem=send_sem.at[last_slot + e - 1],
                    recv_sem=recv_sem.at[last_slot + z],
                    device_id=(near[e] * 4 + y * 2 + x, core),
                    device_id_type=pl.DeviceIdType.MESH,
                )
                move.start()
                sent.append(move)
        else:
            spot = amp_ref.at[core, near[i], y, x]
            pltpu.make_async_remote_copy(
                src_ref=spot, dst_ref=spot, send_sem=send_sem.at[last_slot],
                recv_sem=recv_sem.at[last_slot + near[i]],
                device_id=(near[i] * 4 + y * 2 + x, core),
                device_id_type=pl.DeviceIdType.MESH,
            ).wait_recv()
        from_y[i] = pass_on(near[i], y, x, at_y)
        from_x[i] = pass_on(near[i], y, x, at_x)
        from_core.append(pass_on(near[i], y, x, at_core))

    def cross_over(i):
        from_y[i].wait_recv()
        if i % 2 == 0:
            from_corner[i] = pass_on(near[i], 1 - y, x, at_x)
        from_core.append(pass_on(near[i], 1 - y, x, at_core))
        from_x[i].wait_recv()
        if i % 2 == 1:
            from_corner[i] = pass_on(near[i], y, 1 - x, at_y)
        from_core.append(pass_on(near[i], y, 1 - x, at_core))

    last_slot = send_sem.shape[0] - nz
    from_y, from_x, from_corner, from_core = {}, {}, {}, []
    for i in range(nz):
        fan_out(i)
        if i >= 1:
            cross_over(i - 1)
            if i >= 2:
                from_corner[i - 2].wait_recv()
                from_core.append(pass_on(near[i - 2], 1 - y, 1 - x, at_core))
    cross_over(nz - 1)
    for i in range(nz - 2, nz):
        from_corner[i].wait_recv()
        from_core.append(pass_on(near[i], 1 - y, 1 - x, at_core))
    for move in from_core:
        move.wait_recv()
    for move in sent:
        move.wait_send()
    for store in stores:
        store.wait()


def pair_call(raw, transforms, lists, occ, virt, pattern, half, pad):
    groups, width, aux = raw.shape
    nz = groups // 4
    steps = 2 * nz
    count = transforms.shape[0]
    tile = (pad, pad)
    flat = jnp.swapaxes(transforms, 1, 2).reshape(count * VB, VB)
    vmem = pl.BlockSpec(memory_space=pltpu.VMEM)
    smem = pl.BlockSpec(memory_space=pltpu.SMEM)
    hbm = pl.BlockSpec(memory_space=pl.ANY)
    slots = 2 * steps + nz + (nz - 1) + nz * 7 + nz
    amps, fit = pl.pallas_call(
        functools.partial(pair_kernel, half, nz),
        in_specs=[smem, smem, smem, vmem, vmem, hbm],
        out_specs=[vmem, hbm],
        out_shape=[
            jax.ShapeDtypeStruct((2, nz, 2, 2) + tile, BF16),
            jax.ShapeDtypeStruct((nz, 2, 2, 2 * pad, aux), BF16),
        ],
        scratch_shapes=[
            pltpu.VMEM((count, VB, width), F32),
            pltpu.VMEM((steps, 2, width, aux), BF16),
            pltpu.VMEM((steps, 2, 2 * pad, aux), BF16),
            pltpu.VMEM((2, steps, 2) + tile, BF16),
            pltpu.VMEM((steps, 2) + tile, BF16),
            pltpu.VMEM((steps, 2) + tile, BF16),
            pltpu.VMEM((steps,) + tile, BF16),
            pltpu.VMEM((steps,) + tile, BF16),
            pltpu.VMEM((nz,) + tile, BF16),
            pltpu.VMEM((nz,) + tile, BF16),
            pltpu.VMEM((nz - 1,) + tile, BF16),
            pltpu.SemaphoreType.DMA((steps,)),
            pltpu.SemaphoreType.DMA((steps,)),
            pltpu.SemaphoreType.DMA((slots,)),
            pltpu.SemaphoreType.DMA((slots,)),
        ],
        compiler_params=pltpu.CompilerParams(collective_id=0, has_side_effects=True),
        name="pairs",
    )(
        jnp.transpose(lists, (2, 1, 0)), pattern, occ, virt.T, flat,
        raw.reshape(nz, 2, 2, width, aux),
    )
    return amps.reshape((2, groups) + tile), fit.reshape(groups, 2 * pad, aux)


def gamma_kernel(half, amp_ref, fit_ref, out_ref):
    pad = fit_ref.shape[1] // 2
    row, col = tile_iota(pad)
    for i in range(fit_ref.shape[0]):
        packed = amp_ref[0, i].astype(F32)
        cross = amp_ref[1, i].astype(F32)
        flipped = packed.T
        diag = packed[:, half : half + 1]
        first = jnp.where(row >= col, packed, flipped)
        last = jnp.where(row < col, packed, jnp.where(row == col, diag, flipped))
        top = jnp.concatenate([first, cross], axis=1)[:half]
        bottom = jnp.concatenate([cross.T, last], axis=1)[:half]
        amp = jnp.concatenate([top, bottom], axis=0).astype(BF16)
        out_ref[i] = jnp.dot(amp, fit_ref[i], preferred_element_type=F32).astype(BF16)


def gamma_call(amps, fit, half):
    groups, double, aux = fit.shape
    pad = double // 2
    some = 8
    return pl.pallas_call(
        functools.partial(gamma_kernel, half),
        grid=(groups // some,),
        in_specs=[
            pl.BlockSpec((2, some, pad, pad), lambda g: (0, g, 0, 0)),
            pl.BlockSpec((some, double, aux), lambda g: (g, 0, 0)),
        ],
        out_specs=pl.BlockSpec((some, 2 * half, aux), lambda g: (g, 0, 0)),
        out_shape=jax.ShapeDtypeStruct((groups, 2 * half, aux), BF16),
        name="gamma",
    )(amps, fit)


def build_fitted(raw_rows, transforms):
    row_count, group_count, width_all = raw_rows.shape
    block_count = transforms.shape[1]
    shaped = raw_rows.reshape(row_count, group_count, block_count, OB, NDOM, VB)
    mixed = jnp.einsum(
        "pgbomu,gbmuv->pgbomv", shaped, transforms, preferred_element_type=jnp.float32
    )
    return mixed.astype(jnp.bfloat16).reshape(row_count, group_count, width_all)


def on_device(
    integrals, domain_transforms, domain_lists, occ_energies, virt_energies, pair_pattern
):
    group_here = lax.axis_index("occ")
    own_lists = lax.dynamic_index_in_dim(domain_lists, group_here, 0, keepdims=True)
    every_transform = jnp.take(domain_transforms, domain_lists, axis=0)
    fitted_all = build_fitted(integrals, every_transform)
    fitted = lax.all_to_all(fitted_all, "occ", split_axis=1, concat_axis=0, tiled=True)
    aux_rows = fitted.shape[0]
    width_all = fitted.shape[2]
    fitted = fitted.reshape(aux_rows, width_all)
    block_count = pair_pattern.shape[1]
    width_block = width_all // block_count
    block_virt = jnp.take(virt_energies, own_lists[0], axis=0)
    col_energy = (occ_energies[0][:, :, None, None] - block_virt[:, None, :, :]).reshape(width_all)
    pattern_now = pair_pattern[0]
    pattern_float = pattern_now.astype(jnp.float32)
    mask_full = jnp.repeat(jnp.repeat(pattern_float, width_block, axis=0), width_block, axis=1)
    partial_sums = lax.dot_general(
        fitted, fitted, (((0,), (0,)), ((), ())), preferred_element_type=jnp.float32
    )
    row_sums = lax.psum_scatter(partial_sums, "blk", scatter_dimension=0, tiled=True)
    share_rows = row_sums.shape[0]
    block_here = lax.axis_index("blk")
    row_energy = lax.dynamic_slice_in_dim(col_energy, block_here * share_rows, share_rows, 0)
    row_mask = lax.dynamic_slice_in_dim(mask_full, block_here * share_rows, share_rows, 0)
    row_amplitudes = (row_mask * row_sums / (row_energy[:, None] + col_energy[None, :])).astype(
        jnp.bfloat16
    )
    amplitudes = lax.all_gather(row_amplitudes, "blk", axis=0, tiled=True)
    gamma_rows = lax.dot_general(
        fitted, amplitudes, (((1,), (1,)), ((), ())), preferred_element_type=jnp.float32
    )
    gamma_rows = gamma_rows.astype(jnp.bfloat16).reshape(aux_rows, 1, width_all)
    return lax.all_to_all(gamma_rows, "occ", split_axis=0, concat_axis=1, tiled=True)


def local_sums(
    integrals, domain_transforms, domain_lists, occ_energies, virt_energies, pair_pattern
):
    width = integrals.shape[2]
    half = width // 2
    pad = -(-half // LANES) * LANES
    amps, fit = pair_call(
        jnp.transpose(integrals, (1, 2, 0)), domain_transforms, domain_lists,
        occ_energies.reshape(2), virt_energies, pair_pattern[0], half, pad,
    )
    return jnp.transpose(gamma_call(amps, fit, half), (2, 0, 1))


def sums_are_smaller(mesh, integrals, pair_pattern):
    rows = integrals.shape[0] // mesh.size
    groups, width = integrals.shape[1:]
    half = width // 2
    return (
        width <= rows
        and rows % LANES == 0
        and pair_pattern.shape[1] == 2
        and mesh.shape["blk"] == 2
        and mesh.shape["occ"] == groups
        and groups % 4 == 0
        and groups >= 8
        and half % VB == 0
        and half % LANES != 0
        and half < LANES
    )


def solution(mesh):
    def program(*args):
        body = local_sums if sums_are_smaller(mesh, args[0], args[5]) else on_device
        return jax.shard_map(
            body,
            mesh=mesh,
            in_specs=(
                P(("occ", "blk"), None, None),
                P(),
                P(),
                P("occ", None, None),
                P(),
                P("occ", None, None),
            ),
            out_specs=P(("occ", "blk"), None, None),
            check_vma=False,
        )(*args)

    return program
```

```python
import functools

import jax
import jax.numpy as jnp
from jax import lax
from jax.experimental import pallas as pl
from jax.experimental.pallas import tpu as pltpu
from jax.sharding import PartitionSpec as P

VB = 24
NDOM = 5
OB = 1
LANES = 128
F32 = jnp.float32
BF16 = jnp.bfloat16
NT = (((1,), (1,)), ((), ()))


def tile_iota(size):
    row = lax.broadcasted_iota(jnp.int32, (size, size), 0)
    col = lax.broadcasted_iota(jnp.int32, (size, size), 1)
    return row, col


def pair_kernel(half, nz, lists_ref, pattern_ref, occ_ref, virt_ref, trans_ref, raw_ref,
                amp_ref, fit_out, turn_ref, wide_ref, raw_buf, fit_buf, parts, got_core, sum_core,
                got_x, sum_x, got_y, sum_y, got_z, in_sem, out_sem, send_sem, recv_sem):
    core = lax.axis_index("blk")
    here = lax.axis_index("occ")
    x = lax.rem(here, 2)
    y = lax.rem(lax.div(here, 2), 2)
    z = lax.div(here, 4)
    at_core = (here, 1 - core)
    at_x = (here + 1 - 2 * x, core)
    at_y = (here + 2 - 4 * y, core)

    def plane(d):
        return lax.rem(z + d, nz)

    def at_z(d):
        return (plane(d) * 4 + y * 2 + x, core)

    steps = 2 * nz
    width = raw_ref.shape[3]
    pad = parts.shape[-1]
    blocks = width // VB

    def place(s):
        return plane(s // 2 + 1), lax.rem(y + 1 + s % 2, 2)

    loads = []
    for s in range(steps):
        zr, yr = place(s)
        loads.append(pltpu.make_async_copy(raw_ref.at[zr, yr], raw_buf.at[s], in_sem.at[s]))
        loads[-1].start()

    barrier = pltpu.get_barrier_semaphore()
    peers = [at_core, at_x, at_y] + [at_z(d) for d in range(1, nz)]
    for peer in peers:
        pl.semaphore_signal(barrier, inc=1, device_id=peer, device_id_type=pl.DeviceIdType.MESH)

    spread_row = lax.broadcasted_iota(jnp.int32, (VB, width), 0)
    spread_col = lax.broadcasted_iota(jnp.int32, (VB, width), 1)
    spread = (lax.rem(spread_col, VB) == spread_row).astype(BF16)
    turn_ref[...] = trans_ref[...].astype(F32)
    for v in range(VB):
        wide_ref[:, v, :] = lax.dot_general(
            turn_ref[:, v, :].astype(BF16), spread, (((0,), (0,)), ((), ())),
            preferred_element_type=F32,
        )
    lane_block = lax.div(spread_col, VB)
    row, col = tile_iota(pad)

    def pair_scale():
        virt = virt_ref[...]
        domain = lax.broadcasted_iota(jnp.int32, virt.shape, 1)
        columns = []
        for h in range(2):
            pieces = []
            for j in range(blocks // 2):
                which = lists_ref[j, h, here]
                energy = jnp.sum(jnp.where(domain == which, virt, 0.0), axis=1, keepdims=True)
                pieces.append(occ_ref[h] - energy)
            pieces.append(jnp.full((pad - half, 1), -1.0, F32))
            columns.append(jnp.broadcast_to(jnp.concatenate(pieces, axis=0), (pad, pad)))
        keep = [pattern_ref[i, j].astype(F32) for i, j in ((0, 0), (0, 1), (1, 1))]
        flip = columns[1].T
        scale = jnp.where(row >= col, keep[0] / (columns[0] + columns[0].T),
                          keep[2] / (columns[1] + flip))
        scale = jnp.where(col == half, keep[2] / (columns[1] + columns[1]), scale)
        return jnp.where(core == 0, scale, keep[1] / (columns[0] + flip))

    sent = []
    slots = iter(range(10**6))

    def copy(source, target, peer):
        slot = next(slots)
        move = pltpu.make_async_remote_copy(
            src_ref=source, dst_ref=target, send_sem=send_sem.at[slot],
            recv_sem=recv_sem.at[slot], device_id=peer,
            device_id_type=pl.DeviceIdType.MESH,
        )
        move.start()
        sent.append(move)
        return move

    def compute(s):
        loads[s].wait()
        zr, yr = place(s)
        for side in range(2):
            group = zr * 4 + yr * 2 + side
            rows = []
            for block in range(blocks):
                h, j = divmod(block, blocks // 2)
                which = lists_ref[j, h, group]
                rows.append(jnp.where(lane_block == block, wide_ref[which], 0.0))
                if (block + 1) * 2 % blocks == 0:
                    rows.append(jnp.zeros((pad - half, width), F32))
            mixer = jnp.concatenate(rows, axis=0).astype(BF16)
            fit = jnp.dot(mixer, raw_buf[s, side], preferred_element_type=F32).astype(BF16)
            fit_buf[s, side] = fit
            sums = lax.dot_general(fit, fit, NT, preferred_element_type=F32)
            first, last = sums[:pad, :pad], sums[pad:, pad:]
            diag = jnp.sum(jnp.where(row == col, last, 0.0), axis=1, keepdims=True)
            packed = jnp.where(row >= col, first, last)
            parts[0, s, side] = jnp.where(col == half, diag, packed).astype(BF16)
            parts[1, s, side] = sums[:pad, pad:].astype(BF16)
        store = pltpu.make_async_copy(fit_buf.at[s], fit_out.at[zr, yr], out_sem.at[s])
        store.start()
        return store

    def add(left, right):
        return (left.astype(F32) + right.astype(F32)).astype(BF16)

    stores, by_core, by_x, by_y, by_z = [], {}, {}, {}, {}
    events = [(t, 0, "fit", t) for t in range(steps)]
    events += [(s + 1, 1, "x", s) for s in range(steps)]
    events += [(s + 4, 2, "z", s) for s in range(1, steps, 2)]
    events += [(s + 3, 3, "y", s) for s in range(steps)]
    for _, _, stage, s in sorted(events):
        if stage == "fit":
            stores.append(compute(s))
            if s == 0:
                pl.semaphore_wait(barrier, len(peers))
            by_core[s] = copy(parts.at[1 - core, s], got_core.at[s], at_core)
            if s == steps - 1:
                scale = pair_scale()
        elif stage == "x":
            by_core[s].wait_recv()
            sum_core[s] = add(parts[core, s], got_core[s])
            by_x[s] = copy(sum_core.at[s, 1 - x], got_x.at[s], at_x)
        elif stage == "y":
            by_x[s].wait_recv()
            sum_x[s] = add(sum_core[s, x], got_x[s])
            if s % 2 == 0:
                by_y[s // 2] = copy(sum_x.at[s], got_y.at[s // 2], at_y)
        else:
            d = s // 2
            by_y[d].wait_recv()
            sum_y[d] = add(sum_x[s], got_y[d])
            if d < nz - 1:
                by_z[d] = copy(sum_y.at[d], got_z.at[d], at_z(d + 1))
    total = sum_y[nz - 1].astype(F32)
    for d in range(nz - 1):
        by_z[d].wait_recv()
        total += got_z[d].astype(F32)
    amp_ref[core, z, y, x] = (total * scale).astype(BF16)

    near = [z]
    low, high = z - 1, z + 1
    for i in range(1, nz):
        rise = jnp.logical_and(high < nz, jnp.logical_or(low < 0, high - z <= z - low))
        near.append(jnp.where(rise, high, low))
        low = jnp.where(rise, low, low - 1)
        high = jnp.where(rise, high + 1, high)

    def pass_on(plane, yr, xr, peer):
        spot = amp_ref.at[core, plane, yr, xr]
        return copy(spot, spot, peer)

    def fan_out(i):
        if i == 0:
            for e in range(nz - 1, 0, -1):
                spot = amp_ref.at[core, z, y, x]
                move = pltpu.make_async_remote_copy(
                    src_ref=spot, dst_ref=spot, send_sem=send_sem.at[last_slot + e - 1],
                    recv_sem=recv_sem.at[last_slot + z],
                    device_id=(near[e] * 4 + y * 2 + x, core),
                    device_id_type=pl.DeviceIdType.MESH,
                )
                move.start()
                sent.append(move)
        else:
            spot = amp_ref.at[core, near[i], y, x]
            pltpu.make_async_remote_copy(
                src_ref=spot, dst_ref=spot, send_sem=send_sem.at[last_slot],
                recv_sem=recv_sem.at[last_slot + near[i]],
                device_id=(near[i] * 4 + y * 2 + x, core),
                device_id_type=pl.DeviceIdType.MESH,
            ).wait_recv()
        from_y[i] = pass_on(near[i], y, x, at_y)
        from_x[i] = pass_on(near[i], y, x, at_x)
        from_core.append(pass_on(near[i], y, x, at_core))

    def cross_over(i):
        from_y[i].wait_recv()
        if i % 2 == 0:
            from_corner[i] = pass_on(near[i], 1 - y, x, at_x)
        from_core.append(pass_on(near[i], 1 - y, x, at_core))
        from_x[i].wait_recv()
        if i % 2 == 1:
            from_corner[i] = pass_on(near[i], y, 1 - x, at_y)
        from_core.append(pass_on(near[i], y, 1 - x, at_core))

    last_slot = send_sem.shape[0] - nz
    from_y, from_x, from_corner, from_core = {}, {}, {}, []
    for i in range(nz):
        fan_out(i)
        if i >= 1:
            cross_over(i - 1)
            if i >= 2:
                from_corner[i - 2].wait_recv()
                from_core.append(pass_on(near[i - 2], 1 - y, 1 - x, at_core))
    cross_over(nz - 1)
    for i in range(nz - 2, nz):
        from_corner[i].wait_recv()
        from_core.append(pass_on(near[i], 1 - y, 1 - x, at_core))
    for move in from_core:
        move.wait_recv()
    for move in sent:
        move.wait_send()
    for store in stores:
        store.wait()


def pair_call(raw, transforms, lists, occ, virt, pattern, half, pad):
    groups, width, aux = raw.shape
    nz = groups // 4
    steps = 2 * nz
    count = transforms.shape[0]
    tile = (pad, pad)
    vmem = pl.BlockSpec(memory_space=pltpu.VMEM)
    smem = pl.BlockSpec(memory_space=pltpu.SMEM)
    hbm = pl.BlockSpec(memory_space=pl.ANY)
    slots = 2 * steps + nz + (nz - 1) + nz * 7 + nz
    amps, fit = pl.pallas_call(
        functools.partial(pair_kernel, half, nz),
        in_specs=[smem, smem, smem, vmem, vmem, hbm],
        out_specs=[vmem, hbm],
        out_shape=[
            jax.ShapeDtypeStruct((2, nz, 2, 2) + tile, BF16),
            jax.ShapeDtypeStruct((nz, 2, 2, 2 * pad, aux), BF16),
        ],
        scratch_shapes=[
            pltpu.VMEM((VB, VB, count), F32),
            pltpu.VMEM((count, VB, width), F32),
            pltpu.VMEM((steps, 2, width, aux), BF16),
            pltpu.VMEM((steps, 2, 2 * pad, aux), BF16),
            pltpu.VMEM((2, steps, 2) + tile, BF16),
            pltpu.VMEM((steps, 2) + tile, BF16),
            pltpu.VMEM((steps, 2) + tile, BF16),
            pltpu.VMEM((steps,) + tile, BF16),
            pltpu.VMEM((steps,) + tile, BF16),
            pltpu.VMEM((nz,) + tile, BF16),
            pltpu.VMEM((nz,) + tile, BF16),
            pltpu.VMEM((nz - 1,) + tile, BF16),
            pltpu.SemaphoreType.DMA((steps,)),
            pltpu.SemaphoreType.DMA((steps,)),
            pltpu.SemaphoreType.DMA((slots,)),
            pltpu.SemaphoreType.DMA((slots,)),
        ],
        compiler_params=pltpu.CompilerParams(collective_id=0, has_side_effects=True),
        name="pairs",
    )(
        jnp.transpose(lists, (2, 1, 0)), pattern, occ, virt.T,
        jnp.transpose(transforms, (1, 2, 0)),
        raw.reshape(nz, 2, 2, width, aux),
    )
    return amps.reshape((2, groups) + tile), fit.reshape(groups, 2 * pad, aux)


def gamma_kernel(half, amp_ref, fit_ref, out_ref):
    pad = fit_ref.shape[1] // 2
    row, col = tile_iota(pad)
    for i in range(fit_ref.shape[0]):
        packed = amp_ref[0, i].astype(F32)
        cross = amp_ref[1, i].astype(F32)
        flipped = packed.T
        diag = packed[:, half : half + 1]
        first = jnp.where(row >= col, packed, flipped)
        last = jnp.where(row < col, packed, jnp.where(row == col, diag, flipped))
        top = jnp.concatenate([first, cross], axis=1)[:half]
        bottom = jnp.concatenate([cross.T, last], axis=1)[:half]
        amp = jnp.concatenate([top, bottom], axis=0).astype(BF16)
        out_ref[i] = jnp.dot(amp, fit_ref[i], preferred_element_type=F32).astype(BF16)


def gamma_call(amps, fit, half):
    groups, double, aux = fit.shape
    pad = double // 2
    some = groups // 2
    return pl.pallas_call(
        functools.partial(gamma_kernel, half),
        grid=(groups // some,),
        in_specs=[
            pl.BlockSpec((2, some, pad, pad), lambda g: (0, g, 0, 0)),
            pl.BlockSpec((some, double, aux), lambda g: (g, 0, 0)),
        ],
        out_specs=pl.BlockSpec((some, 2 * half, aux), lambda g: (g, 0, 0)),
        out_shape=jax.ShapeDtypeStruct((groups, 2 * half, aux), BF16),
        name="gamma",
    )(amps, fit)


def build_fitted(raw_rows, transforms):
    row_count, group_count, width_all = raw_rows.shape
    block_count = transforms.shape[1]
    shaped = raw_rows.reshape(row_count, group_count, block_count, OB, NDOM, VB)
    mixed = jnp.einsum(
        "pgbomu,gbmuv->pgbomv", shaped, transforms, preferred_element_type=jnp.float32
    )
    return mixed.astype(jnp.bfloat16).reshape(row_count, group_count, width_all)


def on_device(
    integrals, domain_transforms, domain_lists, occ_energies, virt_energies, pair_pattern
):
    group_here = lax.axis_index("occ")
    own_lists = lax.dynamic_index_in_dim(domain_lists, group_here, 0, keepdims=True)
    every_transform = jnp.take(domain_transforms, domain_lists, axis=0)
    fitted_all = build_fitted(integrals, every_transform)
    fitted = lax.all_to_all(fitted_all, "occ", split_axis=1, concat_axis=0, tiled=True)
    aux_rows = fitted.shape[0]
    width_all = fitted.shape[2]
    fitted = fitted.reshape(aux_rows, width_all)
    block_count = pair_pattern.shape[1]
    width_block = width_all // block_count
    block_virt = jnp.take(virt_energies, own_lists[0], axis=0)
    col_energy = (occ_energies[0][:, :, None, None] - block_virt[:, None, :, :]).reshape(width_all)
    pattern_now = pair_pattern[0]
    pattern_float = pattern_now.astype(jnp.float32)
    mask_full = jnp.repeat(jnp.repeat(pattern_float, width_block, axis=0), width_block, axis=1)
    partial_sums = lax.dot_general(
        fitted, fitted, (((0,), (0,)), ((), ())), preferred_element_type=jnp.float32
    )
    row_sums = lax.psum_scatter(partial_sums, "blk", scatter_dimension=0, tiled=True)
    share_rows = row_sums.shape[0]
    block_here = lax.axis_index("blk")
    row_energy = lax.dynamic_slice_in_dim(col_energy, block_here * share_rows, share_rows, 0)
    row_mask = lax.dynamic_slice_in_dim(mask_full, block_here * share_rows, share_rows, 0)
    row_amplitudes = (row_mask * row_sums / (row_energy[:, None] + col_energy[None, :])).astype(
        jnp.bfloat16
    )
    amplitudes = lax.all_gather(row_amplitudes, "blk", axis=0, tiled=True)
    gamma_rows = lax.dot_general(
        fitted, amplitudes, (((1,), (1,)), ((), ())), preferred_element_type=jnp.float32
    )
    gamma_rows = gamma_rows.astype(jnp.bfloat16).reshape(aux_rows, 1, width_all)
    return lax.all_to_all(gamma_rows, "occ", split_axis=0, concat_axis=1, tiled=True)


def local_sums(
    integrals, domain_transforms, domain_lists, occ_energies, virt_energies, pair_pattern
):
    width = integrals.shape[2]
    half = width // 2
    pad = -(-half // LANES) * LANES
    amps, fit = pair_call(
        jnp.transpose(integrals, (1, 2, 0)), domain_transforms, domain_lists,
        occ_energies.reshape(2), virt_energies, pair_pattern[0], half, pad,
    )
    return jnp.transpose(gamma_call(amps, fit, half), (2, 0, 1))


def sums_are_smaller(mesh, integrals, pair_pattern):
    rows = integrals.shape[0] // mesh.size
    groups, width = integrals.shape[1:]
    half = width // 2
    return (
        width <= rows
        and rows % LANES == 0
        and pair_pattern.shape[1] == 2
        and mesh.shape["blk"] == 2
        and mesh.shape["occ"] == groups
        and groups % 4 == 0
        and groups >= 8
        and half % VB == 0
        and half % LANES != 0
        and half < LANES
    )


def solution(mesh):
    def program(*args):
        body = local_sums if sums_are_smaller(mesh, args[0], args[5]) else on_device
        return jax.shard_map(
            body,
            mesh=mesh,
            in_specs=(
                P(("occ", "blk"), None, None),
                P(),
                P(),
                P("occ", None, None),
                P(),
                P("occ", None, None),
            ),
            out_specs=P(("occ", "blk"), None, None),
            check_vma=False,
        )(*args)

    return program
```
